32 devices in a mesh: leaf: 8 (over z, x), helper: 4 (over y, core).
Axes of the slice: x: 2, y: 2, z: 4, core: 2. Of those that a mesh axis runs over, the one named last changes fastest.
Arguments:
- charges: bfloat16 [32, 262144], P(None, ('leaf', 'helper')), may hold values from -6 to 6
- leaf_basis: bfloat16 [2048, 64, 128], P(('leaf', 'helper')), may hold values from -0.5 to 0.5
- near_field: bfloat16 [2048, 128, 128], P(('leaf', 'helper')), may hold values from -0.5 to 0.5
- local_transfer: bfloat16 [8, 510, 4096], P('leaf'), may hold values from -0.625 to 0.625
- top_transfer: bfloat16 [14, 4096], replicated, may hold values from -0.625 to 0.625
- top_coupling: bfloat16 [14, 4096], replicated, may hold values from -0.75 to 0.75
- leaf_coupling: bfloat16 [8, 4096, 64, 64], P('leaf', 'helper'), may hold values from -0.75 to 0.75
- task_target: int32 [8, 4096], P('leaf', 'helper'), may hold values from 0 to 256, as said below
- task_source: int32 [8, 4096], P('leaf', 'helper'), may hold values from 0 to 767, as said below
Outputs:
- potential: bfloat16 [32, 262144], P(None, ('leaf', 'helper'))
The draws below stay inside these ranges and needn't reach their ends.
Inputs may be any that keep to these rules, and one draw needn't show every extreme that they name: `task_target`: on every device of helper the live slots (target below 256) come first and the others hold target 256; each subtree has exactly 2048 live slots, and one device of each subtree has all 1024 of its slots live. `task_source`: A live slot's source names a leaf of an existing subtree: k * 256 + leaf with k = 0 for the previous subtree, 1 for its own, 2 for the next; empty slots hold 0.
All inputs are finite; a program needn't handle non-finite values.
Results may differ from the reference program's by a relative error of at most 0.0058.
Values may be sent and summed in bfloat16 or wider, within the bound.
No kernel may reach another device: no remote copies, remote signals or barrier semaphores. Data moves between devices by JAX's collectives and lax.ppermute only.
A program may use at most 192 MiB of HBM per device.

```python
import jax
import jax.numpy as jnp
from jax import lax

RANK = 64
RHS = 32
LEAF = 128
SLOTS = 1024
GROUPS = 8
GROUP_LEAVES = 256
LEAVES = 2048
POINTS = 262144
N_HELPER = 4


def task_lists(key):
    base_key = jax.random.fold_in(key, 31)
    group_keys = jax.random.split(base_key, GROUPS)
    spare_rows = (N_HELPER // 2 - 1) * SLOTS
    others = (N_HELPER - 1) * SLOTS

    def one_group(group_key, group_position):
        subkeys = jax.random.split(group_key, 5)
        busiest = jax.random.randint(subkeys[0], (), 0, N_HELPER)
        shuffled = jax.random.permutation(subkeys[1], others)
        marked = jnp.zeros((others,), jnp.int32).at[shuffled].set((jnp.arange(others) < spare_rows).astype(jnp.int32))
        other_counts = marked.reshape(N_HELPER - 1, SLOTS).sum(axis=1)
        helpers_all = jnp.arange(N_HELPER)
        shifted = jnp.where(helpers_all > busiest, helpers_all - 1, helpers_all)
        shifted = jnp.minimum(shifted, N_HELPER - 2)
        counts = jnp.where(helpers_all == busiest, SLOTS, other_counts[shifted])
        active = jnp.arange(SLOTS)[None, :] < counts[:, None]
        leaves = jax.random.randint(subkeys[2], (N_HELPER, SLOTS), 0, GROUP_LEAVES)
        lowest = jnp.where(group_position == 0, 1, 0)
        highest = jnp.where(group_position == GROUPS - 1, 2, 3)
        side_index = jax.random.randint(subkeys[3], (N_HELPER, SLOTS), lowest, highest)
        anchors = jax.random.randint(subkeys[4], (N_HELPER, SLOTS), 0, GROUP_LEAVES)
        targets = jnp.where(active, leaves, GROUP_LEAVES)
        sources = jnp.where(active, side_index * GROUP_LEAVES + anchors, 0)
        return (targets.reshape(-1).astype(jnp.int32), sources.reshape(-1).astype(jnp.int32))
    return jax.vmap(one_group)(group_keys, jnp.arange(GROUPS))


def draw_task_target(key, part):
    return task_lists(key)[0]


def draw_task_source(key, part):
    return task_lists(key)[1]


def steps_of(stream_key, dims, pieces, least, top_value):
    factor_of, own = 1.0, jax.random.fold_in(stream_key, 6)
    for position, parts in pieces:
        heights = jnp.exp(jax.random.uniform(jax.random.fold_in(own, position), (parts,), jnp.float32, least / len(pieces), top_value / len(pieces)))
        factor_of = factor_of * jnp.repeat(heights, dims[position] // parts).reshape([-1 if axis == position else 1 for axis in range(len(dims))])
    return factor_of


def noise(own_key, shape, scale, most, cuts=(), dtype=jnp.bfloat16):
    loudness = steps_of(own_key, shape, cuts, -0.22, 0.18) if cuts else 1.0
    drawn = jax.random.normal(own_key, shape, jnp.float32) * scale * loudness
    return jnp.minimum(jnp.maximum(drawn, -most), most).astype(dtype)


def setup_inputs(seed: int = 0) -> dict:
    key_list = jax.random.split(jax.random.key(seed), 10)
    charges = noise(key_list[0], (RHS, POINTS), 1.0, 6.0, ((1, 32),))
    leaf_basis = noise(key_list[1], (LEAVES, RANK, LEAF), LEAF ** -0.5, 0.5, ((0, 32),))
    near_field = noise(key_list[2], (LEAVES, LEAF, LEAF), LEAF ** -0.5, 0.5, ((0, 32),))
    local_transfer = noise(key_list[3], (GROUPS, 2 * GROUP_LEAVES - 2, RANK * RANK), ((3 * RANK) // 2) ** -0.5, 0.625, ((0, 8),))
    top_transfer = noise(key_list[4], (2 * GROUPS - 2, RANK * RANK), ((3 * RANK) // 2) ** -0.5, 0.625)
    top_coupling = noise(key_list[5], (2 * GROUPS - 2, RANK * RANK), RANK ** -0.5, 0.75)
    leaf_coupling = noise(key_list[6], (GROUPS, N_HELPER * SLOTS, RANK, RANK), RANK ** -0.5, 0.75, ((0, 8), (1, 4)))
    task_target = draw_task_target(jax.random.fold_in(key_list[9], 71), 0)
    task_source = draw_task_source(jax.random.fold_in(key_list[9], 71), 0)
    return {"charges": charges, "leaf_basis": leaf_basis, "near_field": near_field, "local_transfer": local_transfer, "top_transfer": top_transfer, "top_coupling": top_coupling, "leaf_coupling": leaf_coupling, "task_target": task_target, "task_source": task_source}


def couple_group(operands):
    blocks, targets, sources, window = operands
    picked = window[sources].astype(jnp.float32)
    matrices = blocks.reshape(-1, RANK, RANK).astype(jnp.float32)
    products = jnp.einsum('tij,tjr->tir', matrices, picked, precision=lax.Precision.HIGHEST)
    summed = jax.ops.segment_sum(products, targets, num_segments=GROUP_LEAVES + 1)
    return summed[:GROUP_LEAVES]


def reference(charges, leaf_basis, near_field, local_transfer, top_transfer, top_coupling, leaf_coupling, task_target, task_source):
    points = charges.astype(jnp.float32).reshape(RHS, LEAVES, LEAF)
    basis_wide = leaf_basis.astype(jnp.float32)
    leaf_coef = jnp.einsum('lkp,rlp->lkr', basis_wide, points, precision=lax.Precision.HIGHEST).astype(jnp.bfloat16)
    grouped = leaf_coef.reshape(GROUPS, GROUP_LEAVES, RANK, RHS)
    empty_group = jnp.zeros_like(grouped[:1])
    before = jnp.concatenate([empty_group, grouped[:-1]], axis=0)
    after = jnp.concatenate([grouped[1:], empty_group], axis=0)
    window = jnp.concatenate([before, grouped, after], axis=1)
    coupled = lax.map(couple_group, (leaf_coupling, task_target, task_source, window))

    local_mats = local_transfer.astype(jnp.float32).reshape(GROUPS, 2 * GROUP_LEAVES - 2, RANK, RANK)
    current = grouped.astype(jnp.float32)
    offset = 0
    nodes_now = GROUP_LEAVES
    local_levels = []
    while nodes_now > 1:
        matrices = local_mats[:, offset:offset + nodes_now]
        lifted = jnp.einsum('gnij,gnir->gnjr', matrices, current, precision=lax.Precision.HIGHEST)
        current = lifted.reshape(GROUPS, nodes_now // 2, 2, RANK, RHS).sum(axis=2)
        local_levels.append((offset, nodes_now))
        offset = offset + nodes_now
        nodes_now = nodes_now // 2
    current = current[:, 0]

    top_matrices = top_transfer.astype(jnp.float32).reshape(2 * GROUPS - 2, RANK, RANK)
    top_links = top_coupling.astype(jnp.float32).reshape(2 * GROUPS - 2, RANK, RANK)
    offset = 0
    nodes_now = GROUPS
    received = []
    top_levels = []
    while nodes_now > 1:
        sibling = current.reshape(nodes_now // 2, 2, RANK, RHS)[:, ::-1].reshape(nodes_now, RANK, RHS)
        received.append(jnp.einsum('nij,njr->nir', top_links[offset:offset + nodes_now], sibling, precision=lax.Precision.HIGHEST))
        lifted = jnp.einsum('nij,nir->njr', top_matrices[offset:offset + nodes_now], current, precision=lax.Precision.HIGHEST)
        current = lifted.reshape(nodes_now // 2, 2, RANK, RHS).sum(axis=1)
        top_levels.append((offset, nodes_now))
        offset = offset + nodes_now
        nodes_now = nodes_now // 2
    downward = received[-1]
    for height in range(len(top_levels) - 2, -1, -1):
        offset, nodes_now = top_levels[height]
        repeated = jnp.repeat(downward, 2, axis=0)
        downward = received[height] + jnp.einsum('nij,njr->nir', top_matrices[offset:offset + nodes_now], repeated, precision=lax.Precision.HIGHEST)

    downward = downward[:, None]
    for offset, nodes_now in reversed(local_levels):
        repeated = jnp.repeat(downward, 2, axis=1)
        downward = jnp.einsum('gnij,gnjr->gnir', local_mats[:, offset:offset + nodes_now], repeated, precision=lax.Precision.HIGHEST)

    leaf_field = (coupled + downward).astype(jnp.bfloat16).reshape(LEAVES, RANK, RHS)
    far_part = jnp.einsum('lkp,lkr->rlp', basis_wide, leaf_field.astype(jnp.float32), precision=lax.Precision.HIGHEST)
    near_part = jnp.einsum('lpq,rlq->rlp', near_field.astype(jnp.float32), points, precision=lax.Precision.HIGHEST)
    return (far_part + near_part).astype(jnp.bfloat16).reshape(RHS, POINTS)
```

```python
import functools

import jax
import jax.numpy as jnp
from jax import lax
from jax.experimental import pallas as pl
from jax.experimental.pallas import tpu as pltpu
from jax.sharding import PartitionSpec as P

BF = jnp.bfloat16
F32 = jnp.float32
NT = (((1,), (1,)), ((), ()))
NN = (((1,), (0,)), ((), ()))
BLOCK = 128
STEP = 8


def dot(a, b, dims=NN):
    return lax.dot_general(a, b, dims, preferred_element_type=F32)


def cost(flops, size):
    return pl.CostEstimate(flops=flops, bytes_accessed=size, transcendentals=0)


def lane_low(shape, width):
    return lax.broadcasted_iota(jnp.int32, shape, 1) < width


def split_rows(value):
    high = value.astype(BF)
    low = (value - high.astype(F32)).astype(BF)
    return jnp.concatenate([high, low], axis=0)


def precise(value, matrix, dims=NN):
    rows = value.shape[0]
    both = dot(split_rows(value), matrix, dims)
    return both[:rows] + both[rows:]


def coef_kernel(x_ref, basis_ref, out_ref):
    pairs, rhs, wide = out_ref.shape
    leaf = basis_ref.shape[-1]
    low = lane_low((rhs, wide), wide // 2)
    for p in range(pairs):
        first = x_ref[:, 2 * p * leaf : (2 * p + 1) * leaf]
        second = x_ref[:, (2 * p + 1) * leaf : (2 * p + 2) * leaf]
        both = dot(jnp.concatenate([first, second], axis=0), basis_ref[p], NT)
        out_ref[p] = jnp.where(low, both[:rhs], both[rhs:]).astype(BF)


def leaf_coefs(charges, basis_pairs):
    rhs = charges.shape[0]
    pairs, wide, leaf = basis_pairs.shape
    steps = 4
    per = pairs // steps
    return pl.pallas_call(
        coef_kernel,
        grid=(steps,),
        out_shape=jax.ShapeDtypeStruct((pairs, rhs, wide), BF),
        in_specs=[
            pl.BlockSpec((rhs, per * 2 * leaf), lambda b: (0, b)),
            pl.BlockSpec((per, wide, leaf), lambda b: (b, 0, 0)),
        ],
        out_specs=pl.BlockSpec((per, rhs, wide), lambda b: (b, 0, 0)),
        cost_estimate=cost(pairs * 2 * rhs * wide * leaf * 2, 2_000_000),
        name="coefs",
    )(charges, basis_pairs)


def near_kernel(x_ref, near_ref, out_ref):
    leaf = near_ref.shape[-1]
    for k in range(near_ref.shape[0]):
        here = slice(k * leaf, (k + 1) * leaf)
        out_ref[:, here] = dot(x_ref[:, here], near_ref[k], NT)


def near_part(charges, near_field):
    rhs = charges.shape[0]
    leaves, leaf, _ = near_field.shape
    steps = 4
    per = leaves // steps
    return pl.pallas_call(
        near_kernel,
        grid=(steps,),
        out_shape=jax.ShapeDtypeStruct(charges.shape, F32),
        in_specs=[
            pl.BlockSpec((rhs, per * leaf), lambda b: (0, b)),
            pl.BlockSpec((per, leaf, leaf), lambda b: (b, 0, 0)),
        ],
        out_specs=pl.BlockSpec((rhs, per * leaf), lambda b: (0, b)),
        cost_estimate=cost(leaves * rhs * leaf * leaf * 2, 4_000_000),
        name="near",
    )(charges, near_field)


def turn_kernel(in_ref, out_ref, turned):
    rank = in_ref.shape[0]
    tasks = in_ref.shape[2]
    row = lax.broadcasted_iota(jnp.int32, (tasks, tasks), 0)
    col = lax.broadcasted_iota(jnp.int32, (tasks, tasks), 1)
    unit = (row == col).astype(BF)

    @pl.loop(0, rank, step=8)
    def _(start):
        for k in range(8):
            slab = in_ref[start + k]
            twice = jnp.concatenate([slab, slab], axis=0)
            turned[pl.ds(start + k, tasks, stride=rank), :] = dot(unit, twice, NT)

    out_ref[...] = turned[...].astype(BF).reshape(out_ref.shape)


def turn_blocks(blocks):
    rank, _, slots = blocks.shape
    wide = 2 * rank
    return pl.pallas_call(
        turn_kernel,
        grid=(slots // BLOCK,),
        out_shape=jax.ShapeDtypeStruct((slots, rank, wide), BF),
        in_specs=[pl.BlockSpec((rank, rank, BLOCK), lambda b: (0, 0, b))],
        out_specs=pl.BlockSpec((BLOCK, rank, wide), lambda b: (b, 0, 0)),
        scratch_shapes=[pltpu.VMEM((BLOCK * rank, wide), F32)],
        cost_estimate=cost(slots * rank * wide * 256, 24_000_000),
        name="turn",
    )(blocks)


def task_kernel(parts, live_ref, source_ref, target_ref, *rest):
    window_refs = rest[:parts]
    blocks_ref, own_ref, rest_ref, window, sums, sems = rest[parts:]
    pairs, rhs, wide = window_refs[0].shape
    rank = wide // 2
    step = pl.program_id(0)
    tasks = blocks_ref.shape[0]
    copies = [
        pltpu.make_async_copy(ref, window.at[pl.ds(k * pairs, pairs)], sems.at[k])
        for k, ref in enumerate(window_refs)
    ]

    @pl.when(step == 0)
    def _():
        for copy in copies:
            copy.start()
        sums[...] = jnp.zeros_like(sums)
        for copy in copies:
            copy.wait()

    low = lane_low((rhs, wide), rank)
    base = step * tasks
    count = jnp.clip(live_ref[0] - base, 0, tasks)

    @pl.loop(0, (count + STEP - 1) // STEP)
    def _(group):
        found = []
        for k in range(STEP):
            slot = group * STEP + k
            source = source_ref[base + slot]
            pair = window[lax.shift_right_logical(source, 1)]
            keep = low == ((source & 1) == 0)
            lhs = jnp.where(keep, pair, jnp.zeros_like(pair))
            found.append(dot(lhs, blocks_ref[slot], NT))
        for k in range(STEP):
            slot = group * STEP + k
            sums[target_ref[base + slot]] += found[k]

    @pl.when(step == pl.num_programs(0) - 1)
    def _():
        def joined(p):
            return jnp.concatenate([sums[2 * p], sums[2 * p + 1]], axis=1)

        @pl.loop(0, own_ref.shape[0])
        def _(p):
            own_ref[p] = joined(p)

        @pl.loop(0, rest_ref.shape[0])
        def _(p):
            rest_ref[p] = joined(p + own_ref.shape[0]).astype(BF)


def couple(windows, turned, live, sources, targets, group_leaves, own_pairs):
    parts = len(windows)
    pairs, rhs, wide = windows[0].shape
    slots, rank, _ = turned.shape
    rest = group_leaves // 2 - own_pairs
    whole = lambda b, *_: (0, 0, 0)
    grid_spec = pltpu.PrefetchScalarGridSpec(
        num_scalar_prefetch=3,
        grid=(slots // BLOCK,),
        in_specs=[pl.BlockSpec(memory_space=pl.ANY)] * parts
        + [pl.BlockSpec((BLOCK, rank, wide), lambda b, *_: (b, 0, 0))],
        out_specs=[
            pl.BlockSpec((own_pairs, rhs, wide), whole),
            pl.BlockSpec((rest, rhs, wide), whole),
        ],
        scratch_shapes=[
            pltpu.VMEM((parts * pairs, rhs, wide), BF),
            pltpu.VMEM((group_leaves + 8, rhs, rank), F32),
            pltpu.SemaphoreType.DMA((parts,)),
        ],
    )
    return pl.pallas_call(
        functools.partial(task_kernel, parts),
        grid_spec=grid_spec,
        out_shape=[
            jax.ShapeDtypeStruct((own_pairs, rhs, wide), F32),
            jax.ShapeDtypeStruct((rest, rhs, wide), BF),
        ],
        cost_estimate=cost(slots * rhs * rank * wide * 16, 24_000_000),
        name="tasks",
    )(live, sources, targets, *windows, turned)


def up_kernel(coef_ref, mats_ref, top_ref):
    pairs = coef_ref.shape[0]
    nodes = [dot(coef_ref[p], mats_ref[p]) for p in range(pairs)]
    offset = pairs
    while len(nodes) > 1:
        joined = [
            jnp.concatenate([nodes[2 * p], nodes[2 * p + 1]], axis=1)
            for p in range(len(nodes) // 2)
        ]
        nodes = [precise(j, mats_ref[offset + p]) for p, j in enumerate(joined)]
        offset += len(nodes)
    top_ref[...] = nodes[0]


def tree_up(coefs, mats):
    _, rhs, wide = coefs.shape
    return pl.pallas_call(
        up_kernel,
        out_shape=jax.ShapeDtypeStruct((rhs, wide // 2), F32),
        cost_estimate=cost(mats.size * rhs * 16, 2 * mats.size),
        name="up",
    )(coefs, mats)


def root_kernel(nodes_ref, mats_ref, helper_ref, root_ref):
    helper = helper_ref[0]
    nodes = [nodes_ref[k] for k in range(nodes_ref.shape[0])]
    offset = 0
    level = 0
    while len(nodes) > 1:
        home = lax.shift_right_logical(helper, level)
        lifted = [
            precise(node, mats_ref[offset + jnp.bitwise_xor(home, k)])
            for k, node in enumerate(nodes)
        ]
        offset += len(nodes)
        level += 1
        nodes = [lifted[2 * k] + lifted[2 * k + 1] for k in range(len(nodes) // 2)]
    root_ref[...] = nodes[0]


def group_root(nodes, mats, helper):
    _, rhs, rank = nodes.shape
    return pl.pallas_call(
        root_kernel,
        out_shape=jax.ShapeDtypeStruct((rhs, rank), F32),
        in_specs=[
            pl.BlockSpec(memory_space=pltpu.VMEM),
            pl.BlockSpec(memory_space=pltpu.VMEM),
            pl.BlockSpec(memory_space=pltpu.SMEM),
        ],
        cost_estimate=cost(mats.size * rhs * 16, 2 * mats.size),
        name="root",
    )(nodes, mats, helper)


def down_kernel(
    roots_ref, top_ref, link_ref, crown_ref, mats_ref, place_ref, out_ref
):
    group, helper = place_ref[0], place_ref[1]
    nodes = [roots_ref[k] for k in range(roots_ref.shape[0])]
    helpers = (crown_ref.shape[0] + 2) // 2
    offset = 0
    level = 0
    far = []
    moves = []
    while len(nodes) > 1:
        home = lax.shift_right_logical(group, level)
        far.append(precise(nodes[1], link_ref[offset + home], NT))
        moves.append(offset + home)
        lifted = [
            precise(node, top_ref[offset + jnp.bitwise_xor(home, k)])
            for k, node in enumerate(nodes)
        ] if len(nodes) > 2 else []
        offset += len(nodes)
        level += 1
        nodes = [lifted[2 * k] + lifted[2 * k + 1] for k in range(len(lifted) // 2)]
    down = far[-1]
    for t in range(len(far) - 2, -1, -1):
        down = far[t] + precise(down, top_ref[moves[t]], NT)
    level = helpers.bit_length() - 2
    offset = crown_ref.shape[0]
    count = 2
    while count <= helpers:
        offset -= count
        down = precise(down, crown_ref[offset + lax.shift_right_logical(helper, level)], NT)
        level -= 1
        count *= 2
    nodes = [down]
    pairs = out_ref.shape[0]
    rank = down.shape[1]
    offset = mats_ref.shape[0]
    while len(nodes) <= pairs:
        offset -= len(nodes)
        joined = [precise(node, mats_ref[offset + p], NT) for p, node in enumerate(nodes)]
        if len(nodes) == pairs:
            for p, value in enumerate(joined):
                out_ref[p] = value
            break
        nodes = [part for j in joined for part in (j[:, :rank], j[:, rank:])]


def tree_down(roots, top, links, crown, mats, place, pairs):
    _, rhs, rank = roots.shape
    vmem = pl.BlockSpec(memory_space=pltpu.VMEM)
    return pl.pallas_call(
        down_kernel,
        out_shape=jax.ShapeDtypeStruct((pairs, rhs, 2 * rank), F32),
        in_specs=[vmem] * 5 + [pl.BlockSpec(memory_space=pltpu.SMEM)],
        cost_estimate=cost(mats.size * rhs * 16, 2 * mats.size),
        name="down",
    )(roots, top, links, crown, mats, place)


def final_kernel(count, own_ref, *rest):
    added = rest[:count]
    down_ref, basis_ref, near_ref, out_ref = rest[count:]
    pairs, rhs, wide = own_ref.shape
    leaf = basis_ref.shape[-1]
    low = lane_low((rhs, wide), wide // 2)
    for p in range(pairs):
        total = own_ref[p]
        for ref in added:
            total = total + ref[p].astype(F32)
        field = (total + down_ref[p]).astype(BF)
        none = jnp.zeros_like(field)
        lhs = jnp.concatenate(
            [jnp.where(low, field, none), jnp.where(low, none, field)], axis=0
        )
        far = dot(lhs, basis_ref[p])
        for half in range(2):
            here = slice((2 * p + half) * leaf, (2 * p + half + 1) * leaf)
            out_ref[:, here] = (
                far[half * rhs : (half + 1) * rhs] + near_ref[:, here]
            ).astype(BF)


def finish(own, added, down, basis_pairs, near):
    pairs, rhs, wide = own.shape
    leaf = basis_pairs.shape[-1]
    steps = 4
    per = pairs // steps
    pair_spec = pl.BlockSpec((per, rhs, wide), lambda b: (b, 0, 0))
    flat_spec = pl.BlockSpec((rhs, per * 2 * leaf), lambda b: (0, b))
    return pl.pallas_call(
        functools.partial(final_kernel, len(added)),
        grid=(steps,),
        out_shape=jax.ShapeDtypeStruct(near.shape, BF),
        in_specs=[pair_spec] * (2 + len(added))
        + [pl.BlockSpec((per, wide, leaf), lambda b: (b, 0, 0)), flat_spec],
        out_specs=flat_spec,
        cost_estimate=cost(pairs * rhs * wide * leaf * 4, 5_000_000),
        name="final",
    )(own, *added, down, basis_pairs, near)


def xor_move(value, axis, mask):
    count = lax.axis_size(axis)
    return lax.ppermute(value, axis, [(i, i ^ mask) for i in range(count)])


def shards(
    charges,
    leaf_basis,
    near_field,
    local_transfer,
    top_transfer,
    top_coupling,
    leaf_coupling,
    task_target,
    task_source,
):
    helpers = lax.axis_size("helper")
    groups = lax.axis_size("leaf")
    helper = lax.axis_index("helper")
    group = lax.axis_index("leaf")
    own_leaves, rank, leaf = leaf_basis.shape
    group_leaves = own_leaves * helpers
    own_pairs = own_leaves // 2
    bits = helpers.bit_length() - 1

    basis_pairs = leaf_basis.reshape(own_pairs, 2 * rank, leaf)
    own = leaf_coefs(charges, basis_pairs)

    partner = xor_move(own, "leaf", 1)
    beyond = lax.ppermute(
        partner,
        "leaf",
        [(i, i + 2) for i in range(0, groups - 2, 2)]
        + [(i, i - 2) for i in range(3, groups, 2)],
    )

    def spread(block):
        blocks = {0: block}
        for bit in reversed(range(bits)):
            for k in sorted(blocks):
                blocks[k | 1 << bit] = xor_move(blocks[k], "helper", 1 << bit)
        return [blocks[k] for k in range(helpers)]

    windows = spread(own) + spread(partner) + spread(beyond)

    def place_of(leaf_index):
        owner = jnp.bitwise_xor(leaf_index // own_leaves, helper)
        return owner * own_leaves + leaf_index % own_leaves

    targets, sources = task_target[0], task_source[0]
    is_live = targets < group_leaves
    live = jnp.sum(is_live.astype(jnp.int32)).reshape(1)
    side = sources // group_leaves
    near_side = jnp.where(group % 2 == 0, 2, 0)
    slot = jnp.where(side == 1, 0, jnp.where(side == near_side, 1, 2))
    source_place = slot * group_leaves + place_of(sources % group_leaves)
    target_place = jnp.where(is_live, place_of(targets), group_leaves)

    turned = turn_blocks(jnp.transpose(leaf_coupling[0], (1, 2, 0)))
    near = near_part(charges, near_field)

    rows = local_transfer[0]
    picked = []
    offset = 0
    count = group_leaves
    while count > helpers:
        wanted = count // helpers
        picked.append(lax.dynamic_slice_in_dim(rows, offset + helper * wanted, wanted, 0))
        offset += count
        count //= 2
    mats = jnp.concatenate(picked, axis=0).reshape(own_leaves - 1, 2 * rank, rank)
    crown = rows[offset:].reshape(-1, rank, rank)
    top = top_transfer.reshape(-1, rank, rank)
    links = top_coupling.reshape(-1, rank, rank)

    def gather_nodes(node, axis, size):
        nodes = node[None]
        bit = 1
        while bit < size:
            nodes = jnp.concatenate([nodes, xor_move(nodes, axis, bit)], axis=0)
            bit *= 2
        return nodes

    top_node = tree_up(own, mats)
    root = group_root(
        gather_nodes(top_node, "helper", helpers), crown, helper.reshape(1)
    )
    roots = gather_nodes(root, "leaf", groups)
    down = tree_down(
        roots, top, links, crown, mats, jnp.stack([group, helper]), own_pairs
    )

    sums, others = couple(
        windows, turned, live, source_place, target_place, group_leaves, own_pairs
    )
    blocks = {
        k + 1: others[k * own_pairs : (k + 1) * own_pairs] for k in range(helpers - 1)
    }
    added = []
    for bit in range(bits):
        keep = [k for k in range(0, helpers, 2 << bit)]
        send = jnp.concatenate([blocks[k | 1 << bit] for k in keep], axis=0)
        got = xor_move(send, "helper", 1 << bit)
        for place, k in enumerate(keep):
            piece = got[place * own_pairs : (place + 1) * own_pairs]
            if k == 0:
                added.append(piece)
            else:
                blocks[k] = (blocks[k].astype(F32) + piece.astype(F32)).astype(BF)
    return finish(sums, added, down, basis_pairs, near)


def solution(mesh):
    return jax.shard_map(
        shards,
        mesh=mesh,
        in_specs=(
            P(None, ("leaf", "helper")),
            P(("leaf", "helper"), None, None),
            P(("leaf", "helper"), None, None),
            P("leaf", None, None),
            P(),
            P(),
            P("leaf", "helper", None, None),
            P("leaf", "helper"),
            P("leaf", "helper"),
        ),
        out_specs=P(None, ("leaf", "helper")),
        check_vma=False,
    )
```

```python
import functools

import jax
import jax.numpy as jnp
from jax import lax
from jax.experimental import pallas as pl
from jax.experimental.pallas import tpu as pltpu
from jax.sharding import PartitionSpec as P

BF = jnp.bfloat16
F32 = jnp.float32
NT = (((1,), (1,)), ((), ()))
NN = (((1,), (0,)), ((), ()))
BLOCK = 128
STEP = 16


def dot(a, b, dims=NN):
    return lax.dot_general(a, b, dims, preferred_element_type=F32)


def cost(flops, size):
    return pl.CostEstimate(flops=flops, bytes_accessed=size, transcendentals=0)


def limit(mebibytes):
    return pltpu.CompilerParams(vmem_limit_bytes=mebibytes << 20)


def lane_low(shape, width):
    return lax.broadcasted_iota(jnp.int32, shape, 1) < width


def split_rows(value):
    high = value.astype(BF)
    low = (value - high.astype(F32)).astype(BF)
    return jnp.concatenate([high, low], axis=0)


def precise(value, matrix, dims=NN):
    rows = value.shape[0]
    both = dot(split_rows(value), matrix, dims)
    return both[:rows] + both[rows:]


def coef_kernel(x_ref, basis_ref, out_ref):
    pairs, rhs, wide = out_ref.shape
    leaf = basis_ref.shape[-1]
    low = lane_low((rhs, wide), wide // 2)
    for p in range(pairs):
        first = x_ref[:, 2 * p * leaf : (2 * p + 1) * leaf]
        second = x_ref[:, (2 * p + 1) * leaf : (2 * p + 2) * leaf]
        both = dot(jnp.concatenate([first, second], axis=0), basis_ref[p], NT)
        out_ref[p] = jnp.where(low, both[:rhs], both[rhs:]).astype(BF)


def leaf_coefs(charges, basis_pairs):
    rhs = charges.shape[0]
    pairs, wide, leaf = basis_pairs.shape
    steps = 4
    per = pairs // steps
    return pl.pallas_call(
        coef_kernel,
        grid=(steps,),
        out_shape=jax.ShapeDtypeStruct((pairs, rhs, wide), BF),
        in_specs=[
            pl.BlockSpec((rhs, per * 2 * leaf), lambda b: (0, b)),
            pl.BlockSpec((per, wide, leaf), lambda b: (b, 0, 0)),
        ],
        out_specs=pl.BlockSpec((per, rhs, wide), lambda b: (b, 0, 0)),
        cost_estimate=cost(pairs * 2 * rhs * wide * leaf * 2, 2_000_000),
        compiler_params=limit(8),
        name="coefs",
    )(charges, basis_pairs)


def near_kernel(x_ref, near_ref, out_ref):
    leaf = near_ref.shape[-1]
    for k in range(near_ref.shape[0]):
        here = slice(k * leaf, (k + 1) * leaf)
        out_ref[:, here] = dot(x_ref[:, here], near_ref[k], NT)


def near_part(charges, near_field):
    rhs = charges.shape[0]
    leaves, leaf, _ = near_field.shape
    steps = 4
    per = leaves // steps
    return pl.pallas_call(
        near_kernel,
        grid=(steps,),
        out_shape=jax.ShapeDtypeStruct(charges.shape, F32),
        in_specs=[
            pl.BlockSpec((rhs, per * leaf), lambda b: (0, b)),
            pl.BlockSpec((per, leaf, leaf), lambda b: (b, 0, 0)),
        ],
        out_specs=pl.BlockSpec((rhs, per * leaf), lambda b: (0, b)),
        cost_estimate=cost(leaves * rhs * leaf * leaf * 2, 4_000_000),
        compiler_params=limit(8),
        name="near",
    )(charges, near_field)


def shuffle(size, blocks, back=False):
    wide = size * blocks
    row = lax.broadcasted_iota(jnp.int32, (wide, wide), 0)
    col = lax.broadcasted_iota(jnp.int32, (wide, wide), 1)
    if back:
        row, col = col, row
    inside = col % size
    source = 2 * (inside % (size // 2)) + inside // (size // 2) + col - inside
    return (row == source).astype(BF)


def turn_kernel(in_ref, out_ref, turned):
    rank = in_ref.shape[0]
    tasks = in_ref.shape[2]
    pitch = rank + 1
    row = lax.broadcasted_iota(jnp.int32, (tasks, tasks), 0)
    col = lax.broadcasted_iota(jnp.int32, (tasks, tasks), 1)
    unit = (row == col).astype(BF)

    @pl.loop(0, rank // 8)
    def _(step):
        for k in range(8):
            slab = in_ref[step * 8 + k]
            twice = jnp.concatenate([slab, slab], axis=0)
            place = step * 4 + k // 2 + (k % 2) * (rank // 2)
            turned[pl.ds(place, tasks, stride=pitch), :] = dot(unit, twice, NT)

    @pl.loop(0, tasks // 8)
    def _(step):
        base = pl.multiple_of(step * 8 * pitch, 8)
        for k in range(8):
            out_ref[step * 8 + k] = turned[pl.ds(base + k * pitch, rank), :].astype(BF)


def turn_blocks(blocks):
    rank, _, slots = blocks.shape
    wide = 2 * rank
    return pl.pallas_call(
        turn_kernel,
        grid=(slots // BLOCK,),
        out_shape=jax.ShapeDtypeStruct((slots, rank, wide), BF),
        in_specs=[pl.BlockSpec((rank, rank, BLOCK), lambda b: (0, 0, b))],
        out_specs=pl.BlockSpec((BLOCK, rank, wide), lambda b: (b, 0, 0)),
        scratch_shapes=[pltpu.VMEM((BLOCK * (rank + 1), wide), F32)],
        cost_estimate=cost(slots * rank * wide * 256, 24_000_000),
        compiler_params=limit(16),
        name="turn",
    )(blocks)


def task_kernel(parts, helpers, *refs):
    live_ref, source_ref, target_ref = refs[:3]
    window_refs = refs[3 : 3 + parts]
    blocks_ref, own_ref, send_ref, kept_ref, window, sums, more, ahead, later = refs[
        3 + parts :
    ]
    pairs, rhs, wide = window_refs[0].shape
    rank = wide // 2
    leaves = 2 * pairs * helpers
    low = lane_low((rhs, wide), rank)

    for k, ref in enumerate(window_refs):

        @pl.loop(0, pairs // 8)
        def _(step):
            for j in range(8):
                p = step * 8 + j
                pair = ref[p]
                none = jnp.zeros_like(pair)
                window[2 * (p + k * pairs)] = jnp.where(low, pair, none)
                window[2 * (p + k * pairs) + 1] = jnp.where(low, none, pair)

    @pl.loop(0, sums.shape[0] // 8)
    def _(step):
        for j in range(8):
            sums[step * 8 + j] = jnp.zeros(sums.shape[1:], F32)
            more[step * 8 + j] = jnp.zeros(sums.shape[1:], F32)

    later[...] = jnp.zeros_like(later)

    def product(slot):
        return dot(window[source_ref[slot]], blocks_ref[slot], NT)

    def add(buffer, first, valid):
        for k in range(STEP):
            place = target_ref[jnp.maximum(first, 0) + k]
            if valid is not None:
                place = jnp.where(valid, place, leaves)
            into = sums if k % 2 == 0 else more
            into[place] += buffer[k]

    count = (live_ref[0] + 2 * STEP - 1) // (2 * STEP)

    @pl.loop(0, count)
    def _(group):
        first = group * 2 * STEP
        for k in range(STEP):
            ahead[k] = product(first + k)
        add(later, first - STEP, group > 0)
        for k in range(STEP):
            later[k] = product(first + STEP + k)
        add(ahead, first, None)

    add(later, count * 2 * STEP - STEP, count > 0)

    def joined(p):
        return jnp.concatenate(
            [sums[2 * p] + more[2 * p], sums[2 * p + 1] + more[2 * p + 1]], axis=1
        )

    sent = kept = 0
    for block in range(helpers):
        if block == 0:
            ref, start = own_ref, 0
        elif block % 2:
            ref, start, sent = send_ref, sent * pairs, sent + 1
        else:
            ref, start, kept = kept_ref, kept * pairs, kept + 1

        @pl.loop(0, pairs // 8)
        def _(step):
            for j in range(8):
                p = step * 8 + j
                ref[start + p] = joined(block * pairs + p).astype(ref.dtype)


def couple(windows, turned, live, sources, targets, helpers):
    parts = len(windows)
    pairs, rhs, wide = windows[0].shape
    slots, rank, _ = turned.shape
    vmem = pl.BlockSpec(memory_space=pltpu.VMEM)
    smem = pl.BlockSpec(memory_space=pltpu.SMEM)
    shape = lambda blocks, kind: jax.ShapeDtypeStruct((blocks * pairs, rhs, wide), kind)
    acc = pltpu.VMEM((2 * pairs * helpers + 8, rhs, rank), F32)
    held = pltpu.VMEM((STEP, rhs, rank), F32)
    return pl.pallas_call(
        functools.partial(task_kernel, parts, helpers),
        in_specs=[smem] * 3 + [vmem] * (parts + 1),
        out_shape=[
            shape(1, F32),
            shape(helpers // 2, BF),
            shape(max(helpers // 2 - 1, 1), F32),
        ],
        scratch_shapes=[
            pltpu.VMEM((2 * parts * pairs, rhs, wide), BF),
            acc,
            acc,
            held,
            held,
        ],
        cost_estimate=cost(slots * rhs * rank * wide * 16, 24_000_000),
        compiler_params=limit(24),
        name="tasks",
    )(live, sources, targets, *windows, turned)


def level_plan(group_leaves, helpers):
    offset, count, big = 0, group_leaves, []
    while count // helpers >= 8:
        big.append((offset, count // helpers))
        offset += count
        count //= 2
    return big, offset, count


def up_kernel(plan, helper_ref, coef_ref, *refs):
    big, tail_offset, tail_count = plan
    level_refs = refs[: len(big)]
    tail_ref, top_ref, link_ref = refs[len(big) : len(big) + 3]
    node_ref, mats_ref, rest_ref, upper_ref, across_ref, scratch = refs[len(big) + 3 :]
    pairs, rhs, wide = coef_ref.shape
    rank = wide // 2
    helper = helper_ref[0]
    row = lax.broadcasted_iota(jnp.int32, (wide, rank), 0)
    col = lax.broadcasted_iota(jnp.int32, (wide, rank), 1)
    source = 2 * (col % (rank // 2)) + col // (rank // 2)
    first = (row == source).astype(BF)
    second = (row == source + rank).astype(BF)
    tiles = rank // 2
    pitch = tiles + 1

    def expand(rows, into, place, count):
        for s in range(tiles):
            piece = rows[:, wide * s : wide * (s + 1)].astype(F32)
            scratch[pl.ds(s, count, stride=pitch), :] = piece
        flat = jnp.concatenate(
            [scratch[n * pitch : n * pitch + tiles].astype(BF) for n in range(count)], axis=0
        )
        for half, matrix in enumerate((first, second)):
            turned = dot(flat, matrix).astype(BF)
            for n in range(count):
                into[place + n, half * tiles : (half + 1) * tiles] = turned[
                    n * tiles : (n + 1) * tiles
                ]

    def expand_all(ref, into, base, total):
        full = total // 16

        if full > 1:

            @pl.loop(0, full)
            def _(step):
                start = pl.multiple_of(step * 16, 16)
                expand(ref[pl.ds(start, 16), :], into, base + start, 16)

        elif full:
            expand(ref[0:16, :], into, base, 16)
        left = total - 16 * full
        if left:
            expand(ref[16 * full : total, :], into, base + 16 * full, left)

    base = 0
    for ref, (_, wanted) in zip(level_refs, big):
        expand_all(ref, mats_ref, base, wanted)
        base += wanted
    expand_all(tail_ref, rest_ref, 0, rest_ref.shape[0])
    expand_all(top_ref, upper_ref, 0, upper_ref.shape[0])
    expand_all(link_ref, across_ref, 0, across_ref.shape[0])

    coefs = dot(coef_ref[...].reshape(pairs * rhs, wide), shuffle(rank, 2)).astype(BF)
    nodes = [
        dot(coefs[p * rhs : (p + 1) * rhs], mats_ref[2 * p : 2 * p + 2].reshape(wide, rank))
        for p in range(pairs)
    ]
    base = 2 * pairs
    for _, wanted in big[1:]:
        joined = [jnp.concatenate(nodes[k : k + 2], axis=1) for k in range(0, wanted, 2)]
        nodes = [
            precise(j, mats_ref[base + 2 * p : base + 2 * p + 2].reshape(wide, rank))
            for p, j in enumerate(joined)
        ]
        base += wanted
    base = 0
    while len(nodes) > 1:
        wanted = len(nodes)
        joined = [jnp.concatenate(nodes[k : k + 2], axis=1) for k in range(0, wanted, 2)]
        start = base + helper * wanted
        nodes = [
            precise(j, rest_ref[pl.ds(start + 2 * p, 2)].reshape(wide, rank))
            for p, j in enumerate(joined)
        ]
        base += tail_count
        tail_count //= 2
    node_ref[0] = nodes[0]


def tree_up(coefs, rows, top, links, helper, helpers):
    pairs, rhs, wide = coefs.shape
    rank = wide // 2
    total, flat = rows.shape
    plan = level_plan((total + 2) // 2, helpers)
    big, tail_offset, tail_count = plan
    level_spec = lambda offset, wanted: pl.BlockSpec(
        (wanted, flat), lambda b, ref, o=offset // wanted: (o + ref[0], 0)
    )
    whole = lambda shape: pl.BlockSpec(shape, lambda b, ref: (0,) * len(shape))
    near = sum(wanted for _, wanted in big)
    outs = [
        jax.ShapeDtypeStruct((1, rhs, rank), F32),
        jax.ShapeDtypeStruct((near, rank, rank), BF),
        jax.ShapeDtypeStruct((total - tail_offset, rank, rank), BF),
        jax.ShapeDtypeStruct((top.shape[0], rank, rank), BF),
        jax.ShapeDtypeStruct((top.shape[0], rank, rank), BF),
    ]
    return pl.pallas_call(
        functools.partial(up_kernel, plan),
        grid_spec=pltpu.PrefetchScalarGridSpec(
            num_scalar_prefetch=1,
            grid=(1,),
            in_specs=[whole(coefs.shape)]
            + [level_spec(*level) for level in big]
            + [
                pl.BlockSpec(
                    (2 * tail_count, flat),
                    lambda b, ref, o=tail_offset // (2 * tail_count): (o, 0),
                ),
                whole(top.shape),
                whole(links.shape),
            ],
            out_specs=[whole(out.shape) for out in outs],
            scratch_shapes=[pltpu.VMEM((16 * (rank // 2 + 1), wide), F32)],
        ),
        out_shape=outs,
        cost_estimate=cost(1_500_000_000, 6_000_000),
        compiler_params=limit(20),
        name="up",
    )(helper, coefs, *[rows] * (len(big) + 1), top, links)


def listed(refs):
    return [ref[k] for ref in refs for k in range(ref.shape[0])]


def root_kernel(count, start, helper_ref, *refs):
    mats_ref, root_ref = refs[count:]
    helper = helper_ref[0]
    nodes = listed(refs[:count])
    offset = start
    level = 0
    while len(nodes) > 1:
        home = lax.shift_right_logical(helper, level)
        lifted = [
            precise(node, mats_ref[offset + jnp.bitwise_xor(home, k)])
            for k, node in enumerate(nodes)
        ]
        offset += len(nodes)
        level += 1
        nodes = [lifted[2 * k] + lifted[2 * k + 1] for k in range(len(nodes) // 2)]
    root_ref[0] = nodes[0]


def group_root(nodes, mats, helper, helpers):
    vmem = pl.BlockSpec(memory_space=pltpu.VMEM)
    start = mats.shape[0] - (2 * helpers - 2)
    return pl.pallas_call(
        functools.partial(root_kernel, len(nodes), start),
        out_shape=jax.ShapeDtypeStruct((1, *nodes[0].shape[1:]), F32),
        in_specs=[pl.BlockSpec(memory_space=pltpu.SMEM)] + [vmem] * (len(nodes) + 1),
        cost_estimate=cost(50_000_000, 300_000),
        compiler_params=limit(8),
        name="root",
    )(helper, *nodes, mats)


def down_kernel(count, plan, helpers, place_ref, *refs):
    big, _, tail_count = plan
    top_ref, link_ref, rest_ref, mats_ref, out_ref = refs[count:]
    group, helper = place_ref[0], place_ref[1]
    nodes = listed(refs[:count])
    offset = 0
    level = 0
    far = []
    moves = []
    while len(nodes) > 1:
        home = lax.shift_right_logical(group, level)
        far.append(precise(nodes[1], link_ref[offset + home], NT))
        moves.append(offset + home)
        if len(nodes) > 2:
            lifted = [
                precise(node, top_ref[offset + jnp.bitwise_xor(home, k)])
                for k, node in enumerate(nodes)
            ]
        else:
            lifted = []
        offset += len(nodes)
        level += 1
        nodes = [lifted[2 * k] + lifted[2 * k + 1] for k in range(len(lifted) // 2)]
    down = far[-1]
    for t in range(len(far) - 2, -1, -1):
        down = far[t] + precise(down, top_ref[moves[t]], NT)
    rank = down.shape[1]
    wide = 2 * rank
    offset = rest_ref.shape[0]
    length = 2
    while length <= helpers:
        offset -= length
        home = helper // (helpers // length)
        down = precise(down, rest_ref[offset + home], NT)
        length *= 2

    nodes = [down]

    def step(ref, start):
        joined = [
            precise(node, ref[pl.ds(start + 2 * p, 2)].reshape(wide, rank), NT)
            for p, node in enumerate(nodes)
        ]
        return joined

    def halves(joined):
        return [part for j in joined for part in (j[:, :rank], j[:, rank:])]

    while length <= tail_count:
        offset -= length
        wanted = length // helpers
        nodes = halves(step(rest_ref, offset + helper * wanted))
        length *= 2
    offset = mats_ref.shape[0]
    for _, wanted in reversed(big):
        offset -= wanted
        joined = step(mats_ref, offset)
        if offset:
            nodes = halves(joined)
    for p, value in enumerate(joined):
        out_ref[p] = value


def tree_down(roots, top, links, rest, mats, place, pairs, helpers, group_leaves):
    _, rhs, rank = roots[0].shape
    vmem = pl.BlockSpec(memory_space=pltpu.VMEM)
    plan = level_plan(group_leaves, helpers)
    return pl.pallas_call(
        functools.partial(down_kernel, len(roots), plan, helpers),
        out_shape=jax.ShapeDtypeStruct((pairs, rhs, 2 * rank), F32),
        in_specs=[pl.BlockSpec(memory_space=pltpu.SMEM)] + [vmem] * (len(roots) + 4),
        cost_estimate=cost(mats.size * rhs * 16, 4 * mats.size),
        compiler_params=limit(12),
        name="down",
    )(place, *roots, top, links, rest, mats)


def final_kernel(count, own_ref, *rest):
    added = rest[:count]
    down_ref, basis_ref, near_ref, out_ref = rest[count:]
    pairs, rhs, wide = own_ref.shape
    leaf = basis_ref.shape[-1]
    low = lane_low((rhs, wide), wide // 2)
    total = own_ref[...] + down_ref[...]
    for ref in added:
        total = total + ref[...].astype(F32)
    field = total.astype(BF).reshape(pairs * rhs, wide)
    field = dot(field, shuffle(wide // 2, 2, back=True)).astype(BF)
    for p in range(pairs):
        mine = field[p * rhs : (p + 1) * rhs]
        none = jnp.zeros_like(mine)
        lhs = jnp.concatenate(
            [jnp.where(low, mine, none), jnp.where(low, none, mine)], axis=0
        )
        far = dot(lhs, basis_ref[p])
        for half in range(2):
            here = slice((2 * p + half) * leaf, (2 * p + half + 1) * leaf)
            out_ref[:, here] = (
                far[half * rhs : (half + 1) * rhs] + near_ref[:, here]
            ).astype(BF)


def finish(own, added, down, basis_pairs, near):
    pairs, rhs, wide = own.shape
    leaf = basis_pairs.shape[-1]
    steps = 4
    per = pairs // steps
    pair_spec = pl.BlockSpec((per, rhs, wide), lambda b: (b, 0, 0))
    flat_spec = pl.BlockSpec((rhs, per * 2 * leaf), lambda b: (0, b))
    return pl.pallas_call(
        functools.partial(final_kernel, len(added)),
        grid=(steps,),
        out_shape=jax.ShapeDtypeStruct(near.shape, BF),
        in_specs=[pair_spec] * (2 + len(added))
        + [pl.BlockSpec((per, wide, leaf), lambda b: (b, 0, 0)), flat_spec],
        out_specs=flat_spec,
        cost_estimate=cost(pairs * rhs * wide * leaf * 4, 5_000_000),
        compiler_params=limit(12),
        name="final",
    )(own, *added, down, basis_pairs, near)


def xor_move(value, axis, mask):
    count = lax.axis_size(axis)
    return lax.ppermute(value, axis, [(i, i ^ mask) for i in range(count)])


def gather_nodes(node, axis):
    left = lax.axis_size(axis)
    pieces = [node]
    stride = 1
    while left > 1:
        radix = min(8, left)
        payload = pieces[0] if len(pieces) == 1 else jnp.concatenate(pieces, axis=0)
        pieces = [payload] + [xor_move(payload, axis, m * stride) for m in range(1, radix)]
        stride *= radix
        left //= radix
    return pieces


def shards(
    charges,
    leaf_basis,
    near_field,
    local_transfer,
    top_transfer,
    top_coupling,
    leaf_coupling,
    task_target,
    task_source,
):
    helpers = lax.axis_size("helper")
    groups = lax.axis_size("leaf")
    helper = lax.axis_index("helper")
    group = lax.axis_index("leaf")
    own_leaves, rank, leaf = leaf_basis.shape
    group_leaves = own_leaves * helpers
    own_pairs = own_leaves // 2
    bits = helpers.bit_length() - 1

    basis_pairs = leaf_basis.reshape(own_pairs, 2 * rank, leaf)
    own = leaf_coefs(charges, basis_pairs)

    partner = xor_move(own, "leaf", 1)
    beyond = lax.ppermute(
        partner,
        "leaf",
        [(i, i + 2) for i in range(0, groups - 2, 2)]
        + [(i, i - 2) for i in range(3, groups, 2)],
    )

    def spread(block):
        blocks = {0: block}
        for bit in reversed(range(bits)):
            for k in sorted(blocks):
                blocks[k | 1 << bit] = xor_move(blocks[k], "helper", 1 << bit)
        return [blocks[k] for k in range(helpers)]

    windows = spread(own) + spread(partner) + spread(beyond)

    def place_of(leaf_index):
        owner = jnp.bitwise_xor(leaf_index // own_leaves, helper)
        return owner * own_leaves + leaf_index % own_leaves

    targets, sources = task_target[0], task_source[0]
    is_live = targets < group_leaves
    live = jnp.sum(is_live.astype(jnp.int32)).reshape(1)
    side = sources // group_leaves
    near_side = jnp.where(group % 2 == 0, 2, 0)
    slot = jnp.where(side == 1, 0, jnp.where(side == near_side, 1, 2))
    source_place = slot * group_leaves + place_of(sources % group_leaves)
    target_place = jnp.where(is_live, place_of(targets), group_leaves)

    top_node, mats, rest, top, links = tree_up(
        own, local_transfer[0], top_transfer, top_coupling, helper.reshape(1), helpers
    )
    turned = turn_blocks(jnp.transpose(leaf_coupling[0], (1, 2, 0)))
    near = near_part(charges, near_field)
    root = group_root(gather_nodes(top_node, "helper"), rest, helper.reshape(1), helpers)
    down = tree_down(
        gather_nodes(root, "leaf"),
        top,
        links,
        rest,
        mats,
        jnp.stack([group, helper]),
        own_pairs,
        helpers,
        group_leaves,
    )

    sums, sent, kept = couple(windows, turned, live, source_place, target_place, helpers)
    added = []
    for bit in range(bits):
        got = xor_move(sent, "helper", 1 << bit)
        added.append(got)
        if bit + 1 < bits:
            total = kept + got[own_pairs:].astype(F32)
            count = total.shape[0] // own_pairs
            odd = [k for k in range(count) if k % 2 == 0]
            even = [k for k in range(count) if k % 2]
            take = lambda picks: jnp.concatenate(
                [total[k * own_pairs : (k + 1) * own_pairs] for k in picks], axis=0
            )
            sent = take(odd).astype(BF)
            kept = take(even) if even else None
    return finish(sums, added, down, basis_pairs, near)


def solution(mesh):
    return jax.shard_map(
        shards,
        mesh=mesh,
        in_specs=(
            P(None, ("leaf", "helper")),
            P(("leaf", "helper"), None, None),
            P(("leaf", "helper"), None, None),
            P("leaf", None, None),
            P(),
            P(),
            P("leaf", "helper", None, None),
            P("leaf", "helper"),
            P("leaf", "helper"),
        ),
        out_specs=P(None, ("leaf", "helper")),
        check_vma=False,
    )
```
